32 devices in a mesh: ctx: 4 (over z), ep: 8 (over y, x, core).
Axes of the slice: x: 2, y: 2, z: 4, core: 2. Of those that a mesh axis runs over, the one named last changes fastest.
Arguments:
- hidden_in: bfloat16 [8, 512, 7168], P('ep', None, 'ctx'), may hold values from -6 to 6
- expert_ids: int32 [8, 512, 1], P('ep'), may hold values from 0 to 3; in each aligned block of 512 rows (0 to 511, 512 to 1023, ..., all dimensions but the last counted through in order) at most 192 rows name the same one
- route_weight: float32 [8, 512, 1], P('ep'), may hold values from 0.05 to 1
- w_gate: bfloat16 [7168, 4096], P('ctx', 'ep'), may hold values from -0.0625 to 0.0625
- w_up: bfloat16 [7168, 4096], P('ctx', 'ep'), may hold values from -0.0625 to 0.0625
- w_down: bfloat16 [4096, 7168], P('ep', 'ctx'), may hold values from -0.1875 to 0.1875
- queries: bfloat16 [8, 512, 6912], P('ep', 'ctx'), may hold values from -112 to 112
- latents: bfloat16 [8, 512, 512], P('ep', 'ctx'), may hold values from -5 to 5
- rope_keys: bfloat16 [8, 512, 64], P('ep', 'ctx'), may hold values from -5 to 5
- marks: int32 [8, 512], P('ep', 'ctx'), may hold values from 0 to 1, as said below
Outputs:
- moe_out: bfloat16 [8, 512, 7168], P('ep', None, 'ctx')
- context: bfloat16 [8, 512, 6144], P('ep', 'ctx')
The draws below stay inside these ranges and needn't reach their ends.
Inputs may be any that keep to these rules, and one draw needn't show every extreme that they name: `expert_ids`: in each sequence no expert is named by more than 192 pairs; in some sequences one is named by exactly 192. `marks`: in each sequence the positions marked 1 form one run of consecutive positions, all in the first half.
All inputs are finite; a program needn't handle non-finite values.
Results may differ from the reference program's by a relative error of at most 0.02.
Values may be sent and summed in bfloat16 or wider, within the bound.
A program may use at most 128 MiB of HBM per device.

```python
import math
import jax
import jax.numpy as jnp
import numpy as np
from jax import lax

D = 7168
LAT = 512
ROPE = 64
QK_DIM = 192
HEADS = 12
HID = 1024
TOPK = 1
SEQ = 512
SEQS = 8
EXPERTS = 4
CAP = 192


def attention_parts(key):
    base = jax.random.fold_in(key, 4242)
    query_key, latent_key, rope_key = jax.random.split(base, 3)
    query_shape = (SEQS, SEQ, HEADS, LAT + ROPE)
    query_vals = jnp.clip(jax.random.normal(query_key, query_shape, jnp.float32), -5.0, 5.0)
    latent_vals = jnp.clip(jax.random.normal(latent_key, (SEQS, SEQ, LAT), jnp.float32), -5.0, 5.0)
    rope_vals = jnp.clip(jax.random.normal(rope_key, (SEQS, SEQ, ROPE), jnp.float32), -5.0, 5.0)
    return (query_vals.reshape(SEQS, SEQ, HEADS * (LAT + ROPE)), latent_vals, rope_vals)


def draw_queries(key, part):
    return attention_parts(key)[0].astype(jnp.bfloat16)


def draw_latents(key, part):
    return attention_parts(key)[1].astype(jnp.bfloat16)


def draw_rope_keys(key, part):
    return attention_parts(key)[2].astype(jnp.bfloat16)


def draw_marks(key, part):
    start_key, length_key = jax.random.split(jax.random.fold_in(key, 77))
    quarter = SEQ // 4
    starts = jax.random.randint(start_key, (SEQS, 1), 0, quarter + 1)
    spans = jax.random.randint(length_key, (SEQS, 1), 1, quarter + 1)
    positions = jnp.arange(SEQ, dtype=jnp.int32)[None, :]
    inside = (positions >= starts) & (positions < starts + spans)
    return inside.astype(jnp.int32)


def block_levels(rng, dims, cuts, smallest, high):
    def one(position, parts):
        steps = jax.random.uniform(jax.random.fold_in(jax.random.fold_in(rng, 6), position), (parts,), jnp.float32, smallest / len(cuts), high / len(cuts))
        return jnp.repeat(jnp.exp(steps), dims[position] // parts).reshape((-1,) + (1,) * (len(dims) - position - 1))

    gain = one(*cuts[0])
    for cut in cuts[1:]:
        gain = gain * one(*cut)
    return gain


def assign_block(rng, own, number, rows, count, top, most, slope):
    order = jax.random.permutation(rng, count)
    heavy_load, common = portions_of(count, rows * top, most, slope, True), portions_of(count, rows * top, most, slope, False)
    places = jnp.arange(count)

    def named(tallies, rotation):
        used = int((tallies > 0).sum())
        fixed = max(1, used // 4)
        moved = fixed + (places - fixed + rotation * (used - fixed)) % max(1, count - fixed)
        return jnp.zeros((count,), jnp.int32).at[order[jnp.where(places < fixed, places, moved)]].set(jnp.asarray(tallies, jnp.int32))

    tallies = jnp.where(number % 4 == 0, named(heavy_load, number // 4), named(common, number - number // 4 - 1))
    mixed = jax.random.permutation(jax.random.fold_in(own, 3), count)
    source_of, taker = mixed[0:count // 2 * 2:2], mixed[1:count // 2 * 2:2]
    room = jnp.minimum(tallies[source_of] - 1, most - tallies[taker]) // 2
    room = jnp.where((source_of == order[0]) | (taker == order[0]) | (tallies[taker] == 0), 0, jnp.maximum(room, 0))
    moved = jax.random.randint(jax.random.fold_in(own, 4), (count // 2,), 0, 1 << 20) % (room + 1)
    tallies = tallies.at[source_of].add(-moved).at[taker].add(moved)
    labels = jnp.searchsorted(jnp.cumsum(tallies), jnp.arange(rows * top), side="right").astype(jnp.int32)
    listing = labels.reshape(top, rows).T
    listing = listing[jax.random.permutation(jax.random.fold_in(own, 1), rows)]
    rotation = jax.random.randint(jax.random.fold_in(own, 2), (rows, 1), 0, top)
    return jnp.take_along_axis(listing, (jnp.arange(top)[None, :] + rotation) % top, axis=1)


def portions_of(number_of, total, bound, lean, full):
    portions = [(1 << 20) // math.isqrt(grade ** lean) + 1 for grade in range(1, number_of + 1)]
    largest = bound if full else min(bound, max(-(-total // number_of), total * portions[0] // sum(portions)))
    least = 1 if total - largest >= number_of - 1 else 0
    given, surplus = [largest] + [least] * (number_of - 1), total - largest - least * (number_of - 1)
    while surplus > 0:
        candidates = [i for i in range(1, number_of) if given[i] < largest] or [i for i in range(1, number_of) if given[i] < bound]
        whole, left = sum([portions[i] for i in candidates]), surplus
        for i in candidates:
            extra = min(bound - given[i], max(1, left * portions[i] // whole), surplus)
            given[i] = given[i] + extra
            surplus = surplus - extra
    return np.array(given)


def noise(rng, shape, deviation, reach, pieces=(), kind=jnp.bfloat16):
    values = jax.random.normal(rng, shape, jnp.float32) * deviation
    if len(pieces) > 0:
        values = block_levels(rng, shape, pieces, -0.22, 0.18) * values
    return jnp.clip(values, min=-reach, max=reach).astype(kind)


def setup_inputs(seed: int = 0) -> dict:
    arg_keys = jax.random.split(jax.random.key(seed), 11)
    hidden_in = noise(arg_keys[0], (SEQS, SEQ, D), 1.0, 6.0, ((0, 8), (2, 4)))
    expert_ids_keys = jax.random.split(jax.random.fold_in(arg_keys[1], 1), SEQS * SEQ // SEQ)
    expert_ids_turns = jax.random.permutation(jax.random.fold_in(arg_keys[1], 3), SEQS * SEQ // SEQ)
    expert_ids = jax.vmap(lambda own, number: assign_block(jax.random.fold_in(arg_keys[1], 2), own, number, SEQ, EXPERTS, TOPK, CAP, 2))(expert_ids_keys, expert_ids_turns).reshape((SEQS, SEQ, TOPK))
    route_weight = jnp.clip(jnp.exp(math.log(1.0) - 2.9957323 * jax.random.uniform(arg_keys[2], (SEQS, SEQ, TOPK), jnp.float32) ** block_levels(arg_keys[2], (SEQS, SEQ, TOPK), ((0, 8),), -0.2, 0.2)), 0.05, 1.0)
    w_gate = noise(arg_keys[3], (D, EXPERTS * HID), D ** -0.5, 0.0625, ((0, 4), (1, 8)))
    w_up = noise(arg_keys[4], (D, EXPERTS * HID), D ** -0.5, 0.0625, ((0, 4), (1, 8)))
    w_down = noise(arg_keys[5], (EXPERTS * HID, D), HID ** -0.5, 0.1875, ((0, 8), (1, 4)))
    queries = draw_queries(jax.random.fold_in(arg_keys[10], 71), 0)
    latents = draw_latents(jax.random.fold_in(arg_keys[10], 71), 0)
    rope_keys = draw_rope_keys(jax.random.fold_in(arg_keys[10], 71), 0)
    marks = draw_marks(jax.random.fold_in(arg_keys[10], 71), 0)
    return dict(hidden_in=hidden_in, expert_ids=expert_ids, route_weight=route_weight, w_gate=w_gate, w_up=w_up, w_down=w_down, queries=queries, latents=latents, rope_keys=rope_keys, marks=marks)


def attend_sequence(packed):
    query_all, latent_seq, rope_seq, marks_seq = packed
    length = latent_seq.shape[0]
    query_heads = query_all.reshape(length, HEADS, LAT + ROPE).astype(jnp.float32)
    query_lat = query_heads[:, :, :LAT]
    query_rot = query_heads[:, :, LAT:]
    latent_wide = latent_seq.astype(jnp.float32)
    scores = jnp.einsum('qhd,kd->hqk', query_lat, latent_wide)
    scores = scores + jnp.einsum('qhd,kd->hqk', query_rot, rope_seq.astype(jnp.float32))
    scores = scores * (1.0 / math.sqrt(QK_DIM))
    positions = jnp.arange(length, dtype=jnp.int32)
    own_key = positions[None, :] == positions[:, None]
    visible = (positions[None, :] <= positions[:, None]) & ((marks_seq[None, :] == 0) | own_key)
    masked = jnp.where(visible[None], scores, -jnp.inf)
    highest = lax.optimization_barrier(jnp.max(masked, axis=-1, keepdims=True))
    weights = jnp.exp(masked - highest)
    total = lax.optimization_barrier(jnp.sum(weights, axis=-1))
    rounded = lax.optimization_barrier(weights.astype(jnp.bfloat16)).astype(jnp.float32)
    summed = jnp.einsum('hqk,kd->qhd', rounded, latent_wide)
    result = summed / jnp.transpose(total)[:, :, None]
    return result.reshape(length, HEADS * LAT).astype(jnp.bfloat16)

def reference(hidden_in, expert_ids, route_weight, w_gate, w_up, w_down, queries, latents, rope_keys, marks):
    context = lax.map(attend_sequence, (queries, latents, rope_keys, marks))
    pairs = SEQ * TOPK
    flat_ids = expert_ids.reshape(SEQS, pairs)
    flat_weight = route_weight.reshape(SEQS, pairs)
    slot_range = jnp.arange(CAP, dtype=jnp.int32)
    pair_range = jnp.arange(pairs, dtype=jnp.int32)
    seq_range = jnp.arange(SEQS, dtype=jnp.int32)[:, None]
    half = HID // 2

    def one_expert(expert, total):
        expert_id = jnp.asarray(expert).astype(jnp.int32)
        chosen = flat_ids == expert_id
        rank = jnp.cumsum(chosen.astype(jnp.int32), axis=1) - 1
        match = chosen[:, None, :] & (rank[:, None, :] == slot_range[None, :, None])
        filled = jnp.any(match, axis=-1)
        pair_index = lax.optimization_barrier(jnp.sum(jnp.where(match, pair_range[None, None, :], 0), axis=-1)).astype(jnp.int32)
        token_index = (pair_index // TOPK).astype(jnp.int32)
        gathered = jnp.take_along_axis(hidden_in, token_index[:, :, None], axis=1).reshape(SEQS * CAP, D)
        start = (expert_id * HID).astype(jnp.int32)
        gate_cols = lax.dynamic_slice_in_dim(w_gate, start, HID, 1)
        up_cols = lax.dynamic_slice_in_dim(w_up, start, HID, 1)
        down_rows = lax.dynamic_slice_in_dim(w_down, start, HID, 0)
        gate_act = jnp.dot(gathered, gate_cols, preferred_element_type=jnp.float32)
        up_act = jnp.dot(gathered, up_cols, preferred_element_type=jnp.float32)
        hidden = (jax.nn.silu(gate_act) * up_act).astype(jnp.bfloat16)
        first_half = jnp.dot(hidden[:, :half], down_rows[:half], preferred_element_type=jnp.float32).astype(jnp.bfloat16)
        second_half = jnp.dot(hidden[:, half:], down_rows[half:], preferred_element_type=jnp.float32).astype(jnp.bfloat16)
        combined = (first_half.astype(jnp.float32) + second_half.astype(jnp.float32)).reshape(SEQS, CAP, D)
        slot_weight = jnp.take_along_axis(flat_weight, pair_index, axis=1)
        contribution = jnp.where(filled[:, :, None], slot_weight[:, :, None] * combined, 0.0)
        return total.at[seq_range, token_index].add(contribution)
    moe_sum = lax.fori_loop(0, EXPERTS, one_expert, jnp.zeros((SEQS, SEQ, D), jnp.float32))
    return (moe_sum.astype(jnp.bfloat16), context)
```

```python
import functools
import math

import jax
import jax.numpy as jnp
from jax import lax
from jax.experimental import pallas as pl
from jax.experimental.pallas import tpu as pltpu
from jax.sharding import PartitionSpec as P

LAT = 512
ROPE = 64
QK_DIM = 192
CHUNKS = 16
ORDER = (4, 6, 8, 10, 5, 7, 9, 11, 12, 14, 13, 15, 0, 2, 1, 3)
CHAIN = (0, 2, 4, 5)
SPREAD = (8, 7, 6, 5)
SWAP = 2
MESH = pl.DeviceIdType.MESH


def flip(a, b, size):
    out = 0
    step = 1
    while step < size:
        out = out + lax.rem(lax.div(a, step) + lax.div(b, step), 2) * step
        step *= 2
    return out


def pick_of(table, i):
    out = table[0]
    for k in range(1, len(table)):
        out = jnp.where(i == k, table[k], out)
    return out


def expert_kernel(
    chips,
    depth,
    cap,
    split,
    group,
    ids_ref,
    feat_ref,
    weight_ref,
    gate_ref,
    up_ref,
    down_ref,
    query_ref,
    lat_ref,
    rope_ref,
    mark_ref,
    moe_ref,
    ctx_ref,
    gat_ref,
    ret_ref,
    keys_ref,
    seen_ref,
    packed,
    rows,
    part_out,
    part_in,
    hid,
    half_out,
    half_in,
    summed,
    d_send,
    d_recv,
    f_send,
    f_recv,
    c_send,
    c_recv,
    b_send,
    b_recv,
    h_send,
    h_recv,
    r_send,
    r_recv,
    g_send,
    g_recv,
):
    me = lax.axis_index("ep")
    z = lax.axis_index("ctx")
    core = lax.rem(me, 2)
    chip = lax.div(me, 2)
    sibling = me + 1 - 2 * core
    width = feat_ref.shape[1]
    hidden = gate_ref.shape[1]
    quarter = hidden // 2
    n = CHUNKS
    unit = cap // split

    def block(buf, v):
        if group == 1:
            return buf.at[v]
        start = pl.multiple_of(lax.rem(v, group) * unit, unit)
        return buf.at[lax.div(v, group), pl.ds(start, unit)]

    def pair_of(v):
        return lax.div(v, 2 * split) * split + lax.rem(v, split)

    def core_of(v):
        return lax.rem(lax.div(v, split), 2)

    def remote(src, dst, send, recv, **device):
        return pltpu.make_async_remote_copy(
            src_ref=src, dst_ref=dst, send_sem=send, recv_sem=recv,
            device_id=device, device_id_type=MESH,
        )

    def peer(m):
        return 2 * lax.div(m, split) + core

    def dispatch(m):
        h = lax.rem(m, split)
        return remote(
            packed.at[m], block(rows, me * split + h), d_send.at[m], d_recv.at[chip * split + h], ep=peer(m)
        )

    def arrival(m):
        v = peer(m) * split + lax.rem(m, split)
        return remote(packed.at[m], block(rows, v), d_send.at[m], d_recv.at[m], ep=peer(m))

    def forward(v):
        m = pair_of(v)
        return remote(block(rows, v), block(rows, v), f_send.at[m], f_recv.at[m], ep=sibling)

    nexts = (z + 1, z - 1)
    prevs = (z - 1, z + 1)
    places = (z, depth - 1 - z)

    def chain(d, t):
        at = d * n + t
        return remote(part_out.at[at], part_in.at[at], c_send.at[at], c_recv.at[at], ctx=nexts[d])

    def spread(d, t):
        at = d * n + t
        return remote(hid.at[at], hid.at[at], b_send.at[at], b_recv.at[at], ctx=prevs[d])

    def swap(v):
        m = pair_of(v)
        return remote(block(half_out, v), half_in.at[m], h_send.at[m], h_recv.at[m], ep=sibling)

    def back(m):
        h = lax.rem(m, split)
        return remote(
            summed.at[m], ret_ref.at[chip * split + h], r_send.at[m], r_recv.at[chip * split + h], ep=peer(m)
        )

    def home(m):
        return remote(summed.at[m], ret_ref.at[m], r_send.at[m], r_recv.at[m], ep=peer(m))

    def share(o):
        other = lax.rem(z + o, depth)
        return remote(gat_ref.at[z], gat_ref.at[z], g_send.at[o], g_recv.at[o], ctx=other)

    def shared(o):
        other = lax.rem(z + depth - o, depth)
        return remote(gat_ref.at[z], gat_ref.at[other], g_send.at[o], g_recv.at[o], ctx=other)

    barrier = pltpu.get_barrier_semaphore()

    def greet(o, carry):
        pl.semaphore_signal(
            barrier, inc=1, device_id={"ep": 2 * flip(chip, o, chips) + core}, device_id_type=MESH
        )
        return carry

    lax.fori_loop(1, chips, greet, 0)
    pl.semaphore_signal(barrier, inc=1, device_id={"ep": sibling}, device_id_type=MESH)
    for o in range(1, depth):
        pl.semaphore_signal(
            barrier, inc=1, device_id={"ctx": lax.rem(z + o, depth)}, device_id_type=MESH
        )

    bf16, f32 = jnp.bfloat16, jnp.float32
    iota = lax.broadcasted_iota
    query_rows = query_ref.shape[0]
    lanes = gat_ref.shape[2]
    width_k = LAT + ROPE
    eye = iota(jnp.int32, (query_rows, query_rows), 0) == iota(jnp.int32, (query_rows, query_rows), 1)
    mark_col = jnp.sum(jnp.where(eye, mark_ref[...].astype(f32), 0.0), axis=1, keepdims=True)
    for o in range(1, depth):
        @pl.when(o > z)
        def _():
            gat_ref[o] = jnp.zeros((query_rows, lanes), bf16)

    gat_ref[z, :, :LAT] = lat_ref[...]
    gat_ref[z, :, LAT:width_k] = lax.dot_general(
        jnp.where(eye, 1.0, 0.0).astype(bf16), rope_ref[...], (((1,), (1,)), ((), ())),
        preferred_element_type=f32,
    ).astype(bf16)
    gat_ref[z, :, width_k:] = jnp.broadcast_to(mark_col, (query_rows, lanes - width_k)).astype(bf16)

    ids = ids_ref[...]
    tokens = ids.shape[1]
    kinds = max(chips, 16)
    named = iota(jnp.int32, (kinds, tokens), 0) == ids
    earlier = iota(jnp.int32, (tokens, tokens), 0) < iota(jnp.int32, (tokens, tokens), 1)
    counts = jnp.dot(
        jnp.where(named, 1.0, 0.0).astype(bf16),
        jnp.where(earlier, 1.0, 0.0).astype(bf16),
        preferred_element_type=f32,
    )
    rank = jnp.sum(jnp.where(named, counts, 0.0), axis=0, keepdims=True)
    slots = ids * cap + rank.astype(jnp.int32)

    pl.semaphore_wait(barrier, chips + depth - 1)
    for o in range(1, depth):
        @pl.when(z + o < depth)
        def _():
            share(o).start()

    def pack(o, carry):
        j = flip(chip, o, chips)
        index = j * cap + lax.broadcasted_iota(jnp.int32, (cap, tokens), 0)
        pick = jnp.where(index == slots, 1.0, 0.0).astype(jnp.bfloat16)
        chosen = jnp.dot(pick, feat_ref[...], preferred_element_type=jnp.float32)
        for h in range(split):
            packed[j * split + h] = chosen[h * unit:(h + 1) * unit].astype(bf16)

        @pl.when(o < (3 if chips > 4 else chips))
        def _():
            for h in range(split):
                dispatch(j * split + h).start()

        return carry

    lax.fori_loop(1, chips, pack, 0)
    index = chip * cap + lax.broadcasted_iota(jnp.int32, (cap, tokens), 0)
    pick = jnp.where(index == slots, 1.0, 0.0).astype(jnp.bfloat16)
    chosen = jnp.dot(pick, feat_ref[...], preferred_element_type=jnp.float32)
    for h in range(split):
        block(rows, me * split + h)[...] = chosen[h * unit:(h + 1) * unit].astype(bf16)

    first = lax.div(me * split, group)
    if chips == 4:
        order, swap_lag = ORDER, SWAP
    else:
        order, swap_lag = tuple(range(n)), split
    if depth == 4:
        chain_lag, spread_lag = CHAIN, SPREAD
    else:
        chain_lag = tuple(2 * p for p in range(depth))
        spread_lag = tuple(chain_lag[-1] + 2 * (depth - 1 - p) for p in range(depth))
    chain_at = [pick_of(chain_lag, places[d]) for d in range(2)]
    spread_at = [pick_of(spread_lag, places[d]) for d in range(2)]
    down_lag = spread_lag[0]

    def chunk_at(i):
        return flip(first, pick_of(order, i), n)

    heads = query_ref.shape[1] // width_k
    scale = 1.0 / math.sqrt(QK_DIM)

    def prepare():
        for o in range(1, depth):
            @pl.when(z >= o)
            def _():
                shared(o).wait_recv()

        count = depth * query_rows
        keys = gat_ref[...].reshape(count, lanes)
        row = iota(jnp.int32, (lanes, lanes), 0)
        column = iota(jnp.int32, (lanes, lanes), 1)
        even = (row == column) & (row < width_k)
        odd = row == column + (lanes - width_k)
        contract = (((1,), (1,)), ((), ()))
        for a, chosen in ((0, even), (1, odd)):
            pick = jnp.where(chosen, 1.0, 0.0).astype(bf16)
            keys_ref[a] = lax.dot_general(
                pick, keys, contract, preferred_element_type=f32
            ).astype(bf16)
        pick = jnp.where(iota(jnp.int32, (16, lanes), 1) == width_k, 1.0, 0.0).astype(bf16)
        marks = lax.dot_general(pick, keys, contract, preferred_element_type=f32)[:1]
        query_pos = z * query_rows + iota(jnp.int32, (query_rows, count), 0)
        key_pos = iota(jnp.int32, (query_rows, count), 1)
        visible = (key_pos == query_pos) | ((key_pos < query_pos) & (marks < 0.5))
        seen_ref[...] = jnp.where(visible, 0.0, -1e30)

    def attend_pair(pair):
        latents = gat_ref[:, :, :LAT].reshape(depth * query_rows, LAT)
        base = pl.multiple_of(pair * (2 * width_k), 128)
        mask = seen_ref[...]
        for a in range(2):
            shift = a * (2 * width_k - lanes)
            q = query_ref[:, pl.ds(pl.multiple_of(base + shift, 128), lanes)]
            scores = jnp.dot(q, keys_ref[a], preferred_element_type=f32) * scale
            masked = jnp.where(mask < 0.0, -1e30, scores)
            top = jnp.max(masked, axis=1, keepdims=True)
            weight = jnp.where(mask < 0.0, 0.0, jnp.exp(masked - top))
            total = jnp.sum(weight, axis=1, keepdims=True)
            acc = jnp.dot(weight.astype(bf16), latents, preferred_element_type=f32)
            where = pl.multiple_of((2 * pair + a) * LAT, 128)
            ctx_ref[:, pl.ds(where, LAT)] = (acc / total).astype(bf16)

    def step(i, carry):
        @pl.when(i == 1)
        def _():
            prepare()

        @pl.when((i >= 2) & (i < 2 + heads // 2))
        def _():
            attend_pair(i - 2)

        if chips > 4:
            @pl.when(i == 0)
            def _():
                def far(o, carry):
                    j = flip(chip, o, chips)
                    for h in range(split):
                        dispatch(j * split + h).start()
                    return carry

                lax.fori_loop(3, chips, far, 0)

        @pl.when(i < n)
        def _():
            q = chunk_at(i)
            for g in range(group):
                v = q * group + g
                mine = core_of(v) == core

                @pl.when(mine & (lax.div(v, 2 * split) != chip))
                def _():
                    arrival(pair_of(v)).wait_recv()

                @pl.when(mine)
                def _():
                    forward(v).start()

            for g in range(group):
                v = q * group + g

                @pl.when(core_of(v) != core)
                def _():
                    forward(v).wait_recv()

        for d in range(2):
            t = i - chain_at[d]
            lo, hi = d * quarter, (d + 1) * quarter

            @pl.when((t >= 0) & (t < n))
            def _():
                q = chunk_at(t)
                at = d * n + t
                x = rows[q]
                gate = jnp.dot(x, gate_ref[:, lo:hi], preferred_element_type=jnp.float32)
                up = jnp.dot(x, up_ref[:, lo:hi], preferred_element_type=jnp.float32)

                @pl.when(places[d] == 0)
                def _():
                    part_out[at, :, :quarter] = gate.astype(jnp.bfloat16)
                    part_out[at, :, quarter:] = up.astype(jnp.bfloat16)
                    chain(d, t).start()

                @pl.when(places[d] > 0)
                def _():
                    chain(d, t).wait_recv()
                    gate_sum = gate + part_in[at, :, :quarter].astype(jnp.float32)
                    up_sum = up + part_in[at, :, quarter:].astype(jnp.float32)

                    @pl.when(places[d] < depth - 1)
                    def _():
                        part_out[at, :, :quarter] = gate_sum.astype(jnp.bfloat16)
                        part_out[at, :, quarter:] = up_sum.astype(jnp.bfloat16)
                        chain(d, t).start()

                    @pl.when(places[d] == depth - 1)
                    def _():
                        hid[at] = (jax.nn.silu(gate_sum) * up_sum).astype(jnp.bfloat16)
                        spread(d, t).start()

        for d in range(2):
            t = i - spread_at[d]

            @pl.when((t >= 0) & (t < n) & (places[d] < depth - 1))
            def _():
                spread(d, t).wait_recv()

                @pl.when(places[d] > 0)
                def _():
                    spread(d, t).start()

        t = i - down_lag

        @pl.when((t >= 0) & (t < n))
        def _():
            q = chunk_at(t)
            h0 = hid[t]
            h1 = hid[n + t]
            tile = 256
            for w in range(0, width, tile):
                got = jnp.dot(h0, down_ref[:quarter, w:w + tile], preferred_element_type=jnp.float32)
                got = got + jnp.dot(
                    h1, down_ref[quarter:, w:w + tile], preferred_element_type=jnp.float32
                )
                half_out[q, :, w:w + tile] = got.astype(jnp.bfloat16)
            for g in range(group):
                v = q * group + g

                @pl.when(core_of(v) != core)
                def _():
                    swap(v).start()

        t2 = i - down_lag - swap_lag

        @pl.when((t2 >= 0) & (t2 < n))
        def _():
            q = chunk_at(t2)
            for g in range(group):
                v = q * group + g
                m = pair_of(v)
                local = lax.div(m, split) == chip

                @pl.when(core_of(v) == core)
                def _():
                    swap(v).wait_recv()
                    total = block(half_out, v)[...].astype(f32) + half_in[m].astype(f32)
                    summed[m] = total.astype(bf16)

                    @pl.when(jnp.logical_not(local))
                    def _():
                        back(m).start()

                    @pl.when(local)
                    def _():
                        ret_ref[m] = total.astype(bf16)

        return carry

    lax.fori_loop(0, max(n + down_lag + swap_lag, 2 + heads // 2), step, 0)

    def land(o, carry):
        for h in range(split):
            home(flip(chip, o, chips) * split + h).wait_recv()
        return carry

    lax.fori_loop(1, chips, land, 0)
    diagonal = iota(jnp.int32, (tokens, tokens), 0) == iota(jnp.int32, (tokens, tokens), 1)
    slot_col = jnp.sum(jnp.where(diagonal, slots, 0), axis=1, keepdims=True)
    weight_col = jnp.sum(jnp.where(diagonal, weight_ref[...], 0.0), axis=1, keepdims=True)
    pick = jnp.where(iota(jnp.int32, (tokens, chips * cap), 1) == slot_col, 1.0, 0.0).astype(bf16)
    tile = 256
    for w in range(0, width, tile):
        mixed = jnp.dot(
            pick,
            ret_ref[:, :, w:w + tile].reshape(chips * cap, tile),
            preferred_element_type=f32,
        )
        moe_ref[:, w:w + tile] = (mixed * weight_col).astype(bf16)

    def finish(o, carry):
        j = flip(chip, o, chips)
        for h in range(split):
            dispatch(j * split + h).wait_send()
            back(j * split + h).wait_send()
        return carry

    lax.fori_loop(1, chips, finish, 0)

    def finish_core(j, carry):
        for h in range(split):
            forward((2 * j + core) * split + h).wait_send()
            swap((2 * j + 1 - core) * split + h).wait_send()
        return carry

    lax.fori_loop(0, chips, finish_core, 0)

    def finish_chain(t, carry):
        for d in range(2):
            @pl.when(places[d] < depth - 1)
            def _():
                chain(d, t).wait_send()

            @pl.when(places[d] > 0)
            def _():
                spread(d, t).wait_send()

        return carry

    lax.fori_loop(0, n, finish_chain, 0)
    for o in range(1, depth):
        @pl.when(z + o < depth)
        def _():
            share(o).wait_send()


def expert_call(ids, features, weight, w_gate, w_up, w_down, queries, latents, ropes, marks, chips, depth, cap):
    seq_len, width = features.shape
    hidden = w_gate.shape[1]
    split = max(1, CHUNKS // (2 * chips))
    group = 2 * chips * split // CHUNKS
    n = CHUNKS
    unit = cap // split
    tall = group * unit
    pairs = chips * split
    query_rows = queries.shape[0]
    heads = queries.shape[1] // (LAT + ROPE)
    lanes = -(-(LAT + ROPE + 1) // 128) * 128
    dma = pltpu.SemaphoreType.DMA
    bf16 = jnp.bfloat16
    vmem = pl.BlockSpec(memory_space=pltpu.VMEM)
    return pl.pallas_call(
        functools.partial(expert_kernel, chips, depth, cap, split, group),
        out_shape=(
            jax.ShapeDtypeStruct((seq_len, width), bf16),
            jax.ShapeDtypeStruct((query_rows, heads * LAT), bf16),
        ),
        in_specs=[vmem] * 10,
        out_specs=(vmem, vmem),
        scratch_shapes=[
            pltpu.VMEM((depth, query_rows, lanes), bf16),
            pltpu.VMEM((pairs, unit, width), bf16),
            pltpu.VMEM((2, lanes, depth * query_rows), bf16),
            pltpu.VMEM((query_rows, depth * query_rows), jnp.float32),
            pltpu.VMEM((pairs, unit, width), bf16),
            pltpu.VMEM((n, tall, width), bf16),
            pltpu.VMEM((2 * n, tall, hidden), bf16),
            pltpu.VMEM((2 * n, tall, hidden), bf16),
            pltpu.VMEM((2 * n, tall, hidden // 2), bf16),
            pltpu.VMEM((n, tall, width), bf16),
            pltpu.VMEM((pairs, unit, width), bf16),
            pltpu.VMEM((pairs, unit, width), bf16),
            dma((pairs,)), dma((pairs,)),
            dma((pairs,)), dma((pairs,)),
            dma((2 * n,)), dma((2 * n,)),
            dma((2 * n,)), dma((2 * n,)),
            dma((pairs,)), dma((pairs,)),
            dma((pairs,)), dma((pairs,)),
            dma((depth,)), dma((depth,)),
        ],
        compiler_params=pltpu.CompilerParams(
            collective_id=0, has_side_effects=True, vmem_limit_bytes=60 << 20
        ),
    )(ids, features, weight, w_gate, w_up, w_down, queries, latents, ropes, marks)


def per_device(
    hidden_in, expert_ids, route_weight, w_gate, w_up, w_down, queries, latents, rope_keys, marks
):
    features = hidden_in[0]
    seq_len = features.shape[0]
    slots_per = expert_ids.shape[2]
    chips = lax.axis_size("ep") // 2
    depth = lax.axis_size("ctx")
    capacity = max(2, 3 * seq_len * slots_per // (2 * chips))
    cap = -(-capacity // 16) * 16
    moe, context = expert_call(
        expert_ids[0].reshape(1, -1),
        features,
        route_weight[0].reshape(1, -1),
        w_gate,
        w_up,
        w_down,
        queries[0],
        latents[0],
        jnp.swapaxes(rope_keys, 1, 2)[0],
        marks,
        chips,
        depth,
        cap,
    )
    return (moe[None], context[None])


def solution(mesh):
    placed = (
        P("ep", None, "ctx"),
        P("ep", None, None),
        P("ep", None, None),
        P("ctx", "ep"),
        P("ctx", "ep"),
        P("ep", "ctx"),
        P("ep", "ctx", None),
        P("ep", "ctx", None),
        P("ep", "ctx", None),
        P("ep", "ctx"),
    )
    return jax.shard_map(
        per_device,
        mesh=mesh,
        in_specs=placed,
        out_specs=(P("ep", None, "ctx"), P("ep", "ctx", None)),
        check_vma=False,
    )
```

```python
import functools
import math

import jax
import jax.numpy as jnp
from jax import lax
from jax.experimental import pallas as pl
from jax.experimental.pallas import tpu as pltpu
from jax.sharding import PartitionSpec as P

LAT = 512
ROPE = 64
QK_DIM = 192
CHUNKS = 16
ORDER = (0, 2, 4, 6, 8, 10, 12, 14, 13, 15, 5, 7, 9, 11, 1, 3)
CHAIN = (0, 1, 2, 3)
SPREAD = (6, 5, 4, 3)
SWAP = 2
SUB = 2
RELAY = (2, 4, 6)
ATTEND = 8
DOWN_FIRST = True
MESH = pl.DeviceIdType.MESH


def flip(a, b, size):
    out = 0
    step = 1
    while step < size:
        out = out + lax.rem(lax.div(a, step) + lax.div(b, step), 2) * step
        step *= 2
    return out


def pick_of(table, i):
    out = table[0]
    for k in range(1, len(table)):
        out = jnp.where(i == k, table[k], out)
    return out


def expert_kernel(
    chips,
    depth,
    cap,
    split,
    group,
    ids_ref,
    feat_ref,
    weight_ref,
    gate_hbm,
    up_hbm,
    down_hbm,
    query_hbm,
    lat_ref,
    rope_ref,
    mark_ref,
    ret_ref,
    ctx_hbm,
    pick_hbm,
    scale_hbm,
    gate_ref,
    up_ref,
    down_ref,
    query_ref,
    ctx_ref,
    pick_ref,
    scale_ref,
    gat_ref,
    keys_ref,
    seen_ref,
    packed,
    rows,
    part_out,
    part_in,
    hid,
    half_out,
    half_in,
    summed,
    acc,
    d_send,
    d_recv,
    f_send,
    f_recv,
    c_send,
    c_recv,
    b_send,
    b_recv,
    h_send,
    h_recv,
    r_send,
    r_recv,
    g_send,
    g_recv,
    in_sem,
    out_sem,
    own_sem,
):
    me = lax.axis_index("ep")
    z = lax.axis_index("ctx")
    core = lax.rem(me, 2)
    chip = lax.div(me, 2)
    sibling = me + 1 - 2 * core
    width = feat_ref.shape[1]
    hidden = gate_ref.shape[1]
    quarter = hidden // 2
    n = CHUNKS
    unit = cap // split

    def block(buf, v):
        if group == 1:
            return buf.at[v]
        start = pl.multiple_of(lax.rem(v, group) * unit, unit)
        return buf.at[lax.div(v, group), pl.ds(start, unit)]

    def pair_of(v):
        return lax.div(v, 2 * split) * split + lax.rem(v, split)

    def core_of(v):
        return lax.rem(lax.div(v, split), 2)

    def remote(src, dst, send, recv, **device):
        return pltpu.make_async_remote_copy(
            src_ref=src, dst_ref=dst, send_sem=send, recv_sem=recv,
            device_id=device, device_id_type=MESH,
        )

    def peer(m):
        return 2 * lax.div(m, split) + core

    def dispatch(m):
        h = lax.rem(m, split)
        return remote(
            packed.at[m], block(rows, me * split + h), d_send.at[m], d_recv.at[chip * split + h], ep=peer(m)
        )

    def arrival(m):
        v = peer(m) * split + lax.rem(m, split)
        return remote(packed.at[m], block(rows, v), d_send.at[m], d_recv.at[m], ep=peer(m))

    def forward(v):
        m = pair_of(v)
        return remote(block(rows, v), block(rows, v), f_send.at[m], f_recv.at[m], ep=sibling)

    nexts = (z + 1, z - 1)
    prevs = (z - 1, z + 1)
    places = (z, depth - 1 - z)

    piece = rows.shape[1] // SUB

    def chain(d, t, u):
        at = d * n + t
        cut = pl.ds(u * piece, piece)
        return remote(
            part_out.at[at, cut], part_in.at[at, cut],
            c_send.at[at * SUB + u], c_recv.at[at * SUB + u], ctx=nexts[d],
        )

    def spread(d, t, u):
        at = d * n + t
        cut = pl.ds(u * piece, piece)
        return remote(
            hid.at[at, cut], hid.at[at, cut],
            b_send.at[at * SUB + u], b_recv.at[at * SUB + u], ctx=prevs[d],
        )

    def swap(v):
        m = pair_of(v)
        return remote(block(half_out, v), half_in.at[m], h_send.at[m], h_recv.at[m], ep=sibling)

    def back(m):
        h = lax.rem(m, split)
        return remote(
            summed.at[m], ret_ref.at[chip * split + h], r_send.at[m], r_recv.at[chip * split + h], ep=peer(m)
        )

    def home(m):
        return remote(summed.at[m], ret_ref.at[m], r_send.at[m], r_recv.at[m], ep=peer(m))

    def share(k):
        return remote(gat_ref.at[z - k], gat_ref.at[z - k], g_send.at[k], g_recv.at[k + 1], ctx=z + 1)

    def shared(k):
        return remote(gat_ref.at[z - k], gat_ref.at[z - k], g_send.at[k], g_recv.at[k], ctx=z - 1)

    def relay(k):
        @pl.when(z >= k)
        def _():
            shared(k).wait_recv()

        @pl.when((z >= k) & (z + 1 < depth))
        def _():
            share(k).start()

    loads = [
        pltpu.make_async_copy(src, dst, in_sem.at[k])
        for k, (src, dst) in enumerate(
            ((gate_hbm, gate_ref), (up_hbm, up_ref), (query_hbm, query_ref), (down_hbm, down_ref))
        )
    ]
    for load in loads:
        load.start()
    stores = [
        pltpu.make_async_copy(src, dst, out_sem.at[k])
        for k, (src, dst) in enumerate(((ctx_ref, ctx_hbm), (pick_ref, pick_hbm), (scale_ref, scale_hbm)))
    ]

    def keep(m):
        return pltpu.make_async_copy(summed.at[m], ret_ref.at[m], own_sem.at[lax.rem(m, split)])

    barrier = pltpu.get_barrier_semaphore()

    def greet(o, carry):
        pl.semaphore_signal(
            barrier, inc=1, device_id={"ep": 2 * flip(chip, o, chips) + core}, device_id_type=MESH
        )
        return carry

    lax.fori_loop(1, chips, greet, 0)
    pl.semaphore_signal(barrier, inc=1, device_id={"ep": sibling}, device_id_type=MESH)

    @pl.when(z > 0)
    def _():
        pl.semaphore_signal(barrier, inc=1, device_id={"ctx": z - 1}, device_id_type=MESH)

    @pl.when(z < depth - 1)
    def _():
        pl.semaphore_signal(barrier, inc=1, device_id={"ctx": z + 1}, device_id_type=MESH)

    bf16, f32 = jnp.bfloat16, jnp.float32
    iota = lax.broadcasted_iota
    query_rows = query_ref.shape[0]
    lanes = gat_ref.shape[2]
    width_k = LAT + ROPE
    eye = iota(jnp.int32, (query_rows, query_rows), 0) == iota(jnp.int32, (query_rows, query_rows), 1)
    mark_col = jnp.sum(jnp.where(eye, mark_ref[...].astype(f32), 0.0), axis=1, keepdims=True)
    for o in range(1, depth):
        @pl.when(o > z)
        def _():
            gat_ref[o] = jnp.zeros((query_rows, lanes), bf16)

    gat_ref[z, :, :LAT] = lat_ref[...]
    gat_ref[z, :, LAT:width_k] = lax.dot_general(
        jnp.where(eye, 1.0, 0.0).astype(bf16), rope_ref[...], (((1,), (1,)), ((), ())),
        preferred_element_type=f32,
    ).astype(bf16)
    gat_ref[z, :, width_k:] = jnp.broadcast_to(mark_col, (query_rows, lanes - width_k)).astype(bf16)

    ids = ids_ref[...]
    tokens = ids.shape[1]
    kinds = max(chips, 16)
    named = iota(jnp.int32, (kinds, tokens), 0) == ids
    earlier = iota(jnp.int32, (tokens, tokens), 0) < iota(jnp.int32, (tokens, tokens), 1)
    counts = jnp.dot(
        jnp.where(named, 1.0, 0.0).astype(bf16),
        jnp.where(earlier, 1.0, 0.0).astype(bf16),
        preferred_element_type=f32,
    )
    rank = jnp.sum(jnp.where(named, counts, 0.0), axis=0, keepdims=True)
    slots = ids * cap + rank.astype(jnp.int32)

    pl.semaphore_wait(barrier, chips + jnp.minimum(z, 1) + jnp.minimum(depth - 1 - z, 1))

    @pl.when(z + 1 < depth)
    def _():
        share(0).start()

    def pack(o, carry):
        j = flip(chip, o, chips)
        index = j * cap + lax.broadcasted_iota(jnp.int32, (cap, tokens), 0)
        pick = jnp.where(index == slots, 1.0, 0.0).astype(jnp.bfloat16)
        chosen = jnp.dot(pick, feat_ref[...], preferred_element_type=jnp.float32)
        for h in range(split):
            packed[j * split + h] = chosen[h * unit:(h + 1) * unit].astype(bf16)

        @pl.when(o < (3 if chips > 4 else chips))
        def _():
            for h in range(split):
                dispatch(j * split + h).start()

        return carry

    lax.fori_loop(1, chips, pack, 0)
    index = chip * cap + lax.broadcasted_iota(jnp.int32, (cap, tokens), 0)
    pick = jnp.where(index == slots, 1.0, 0.0).astype(jnp.bfloat16)
    chosen = jnp.dot(pick, feat_ref[...], preferred_element_type=jnp.float32)
    for h in range(split):
        block(rows, me * split + h)[...] = chosen[h * unit:(h + 1) * unit].astype(bf16)

    first = lax.div(me * split, group)
    if chips == 4:
        order, swap_lag = ORDER, SWAP
    else:
        order, swap_lag = tuple(range(n)), split
    if depth == 4:
        chain_lag, spread_lag = CHAIN, SPREAD
    else:
        chain_lag = tuple(2 * p for p in range(depth))
        spread_lag = tuple(chain_lag[-1] + 2 * (depth - 1 - p) for p in range(depth))
    chain_at = [pick_of(chain_lag, places[d]) for d in range(2)]
    spread_at = [pick_of(spread_lag, places[d]) for d in range(2)]
    down_lag = spread_lag[0] + 1

    def chunk_at(i):
        return flip(first, pick_of(order, i), n)

    heads = query_ref.shape[1] // width_k
    scale = 1.0 / math.sqrt(QK_DIM)

    def prepare():
        count = depth * query_rows
        keys = gat_ref[...].reshape(count, lanes)
        row = iota(jnp.int32, (lanes, lanes), 0)
        column = iota(jnp.int32, (lanes, lanes), 1)
        even = (row == column) & (row < width_k)
        odd = row == column + (lanes - width_k)
        contract = (((1,), (1,)), ((), ()))
        for a, chosen in ((0, even), (1, odd)):
            pick = jnp.where(chosen, 1.0, 0.0).astype(bf16)
            keys_ref[a] = lax.dot_general(
                pick, keys, contract, preferred_element_type=f32
            ).astype(bf16)
        pick = jnp.where(iota(jnp.int32, (16, lanes), 1) == width_k, 1.0, 0.0).astype(bf16)
        marks = lax.dot_general(pick, keys, contract, preferred_element_type=f32)[:1]
        query_pos = z * query_rows + iota(jnp.int32, (query_rows, count), 0)
        key_pos = iota(jnp.int32, (query_rows, count), 1)
        visible = (key_pos == query_pos) | ((key_pos < query_pos) & (marks < 0.5))
        seen_ref[...] = jnp.where(visible, 0.0, -1e30)

    def attend(pair, a):
        latents = gat_ref[:, :, :LAT].reshape(depth * query_rows, LAT)
        base = pl.multiple_of(pair * (2 * width_k), 128)
        mask = seen_ref[...]
        shift = a * (2 * width_k - lanes)
        q = query_ref[:, pl.ds(pl.multiple_of(base + shift, 128), lanes)]
        scores = jnp.dot(q, keys_ref[a], preferred_element_type=f32) * scale
        masked = jnp.where(mask < 0.0, -1e30, scores)
        top = jnp.max(masked, axis=1, keepdims=True)
        weight = jnp.where(mask < 0.0, 0.0, jnp.exp(masked - top))
        total = jnp.sum(weight, axis=1, keepdims=True)
        acc = jnp.dot(weight.astype(bf16), latents, preferred_element_type=f32)
        where = pl.multiple_of((2 * pair + a) * LAT, 128)
        ctx_ref[:, pl.ds(where, LAT)] = (acc / total).astype(bf16)

    def combine(i):
        t2 = i - down_lag - swap_lag

        @pl.when((t2 >= 0) & (t2 < n))
        def _():
            q = chunk_at(t2)
            for g in range(group):
                v = q * group + g
                m = pair_of(v)
                local = lax.div(m, split) == chip

                @pl.when(core_of(v) == core)
                def _():
                    swap(v).wait_recv()
                    total = block(half_out, v)[...].astype(f32) + half_in[m].astype(f32)
                    summed[m] = total.astype(bf16)

                    @pl.when(jnp.logical_not(local))
                    def _():
                        back(m).start()

                    @pl.when(local)
                    def _():
                        keep(m).start()

    def arrive(i):
        @pl.when(i < n)
        def _():
            q = chunk_at(i)
            for g in range(group):
                v = q * group + g
                mine = core_of(v) == core

                @pl.when(mine & (lax.div(v, 2 * split) != chip))
                def _():
                    arrival(pair_of(v)).wait_recv()

                @pl.when(mine)
                def _():
                    forward(v).start()

            for g in range(group):
                v = q * group + g

                @pl.when(core_of(v) != core)
                def _():
                    forward(v).wait_recv()

    def project(i, d):
        t = i - chain_at[d]
        lo, hi = d * quarter, (d + 1) * quarter

        @pl.when((t >= 0) & (t < n))
        def _():
            q = chunk_at(t)
            at = d * n + t
            x = rows[q]
            gate = jnp.dot(x, gate_ref[:, lo:hi], preferred_element_type=f32)
            up = jnp.dot(x, up_ref[:, lo:hi], preferred_element_type=f32)

            @pl.when(places[d] == 0)
            def _():
                part_out[at, :, :quarter] = gate.astype(bf16)
                part_out[at, :, quarter:] = up.astype(bf16)

            @pl.when(places[d] > 0)
            def _():
                acc[d, :, :quarter] = gate
                acc[d, :, quarter:] = up

    def pass_on(i, d, u):
        t = i - chain_at[d]
        r0, r1 = u * piece, (u + 1) * piece
        at = d * n + t
        live = (t >= 0) & (t < n)

        @pl.when(live & (places[d] == 0))
        def _():
            chain(d, t, u).start()

        @pl.when(live & (places[d] > 0))
        def _():
            chain(d, t, u).wait_recv()
            total = acc[d, r0:r1] + part_in[at, r0:r1].astype(f32)

            @pl.when(places[d] < depth - 1)
            def _():
                part_out[at, r0:r1] = total.astype(bf16)
                chain(d, t, u).start()

            @pl.when(places[d] == depth - 1)
            def _():
                hid[at, r0:r1] = (jax.nn.silu(total[:, :quarter]) * total[:, quarter:]).astype(bf16)
                spread(d, t, u).start()

    def hand_out(i, d, u):
        t = i - spread_at[d]

        @pl.when((t >= 0) & (t < n) & (places[d] < depth - 1))
        def _():
            spread(d, t, u).wait_recv()

            @pl.when(places[d] > 0)
            def _():
                spread(d, t, u).start()

    def lower(i):
        t = i - down_lag

        @pl.when((t >= 0) & (t < n))
        def _():
            q = chunk_at(t)
            h0 = hid[t]
            h1 = hid[n + t]
            tile = 256
            for w in range(0, width, tile):
                got = jnp.dot(h0, down_ref[:quarter, w:w + tile], preferred_element_type=jnp.float32)
                got = got + jnp.dot(
                    h1, down_ref[quarter:, w:w + tile], preferred_element_type=jnp.float32
                )
                half_out[q, :, w:w + tile] = got.astype(jnp.bfloat16)
            for g in range(group):
                v = q * group + g

                @pl.when(core_of(v) != core)
                def _():
                    swap(v).start()

    def place_rows():
        diagonal = iota(jnp.int32, (tokens, tokens), 0) == iota(jnp.int32, (tokens, tokens), 1)
        slot_col = jnp.sum(jnp.where(diagonal, slots, 0), axis=1, keepdims=True)
        weight_col = jnp.sum(jnp.where(diagonal, weight_ref[...], 0.0), axis=1, keepdims=True)
        where = iota(jnp.int32, (tokens, chips * cap), 1) == slot_col
        pick_ref[...] = jnp.where(where, 1.0, 0.0).astype(bf16)
        scale_ref[...] = jnp.broadcast_to(weight_col, scale_ref.shape)
        stores[1].start()
        stores[2].start()

    def step(i, carry):
        @pl.when(i == ATTEND + heads // 2 + 1)
        def _():
            stores[0].start()
            place_rows()

        for k in range(1, depth):
            @pl.when(i == RELAY[k - 1])
            def _():
                relay(k)

        @pl.when(i == ATTEND)
        def _():
            prepare()

        attending = (i > ATTEND) & (i <= ATTEND + heads // 2)
        arrive(i)
        project(i, 0)
        pass_on(i, 0, 0)
        pass_on(i - 1, 1, 1)
        hand_out(i, 0, 0)
        hand_out(i - 1, 1, 1)

        @pl.when(attending)
        def _():
            attend(i - ATTEND - 1, 0)

        combine(i)
        if DOWN_FIRST:
            lower(i)
        project(i, 1)
        pass_on(i, 0, 1)
        pass_on(i, 1, 0)
        hand_out(i, 0, 1)
        hand_out(i, 1, 0)

        @pl.when(attending)
        def _():
            attend(i - ATTEND - 1, 1)

        if not DOWN_FIRST:
            lower(i)
        return carry

    for load in loads:
        load.wait()
    lax.fori_loop(0, max(n + down_lag + swap_lag, ATTEND + 2 + heads // 2), step, 0)

    def land(o, carry):
        for h in range(split):
            home(flip(chip, o, chips) * split + h).wait_recv()
        return carry

    lax.fori_loop(1, chips, land, 0)
    for h in range(split):
        keep(chip * split + h).wait()
    for store in stores:
        store.wait()

    def finish(o, carry):
        j = flip(chip, o, chips)
        for h in range(split):
            dispatch(j * split + h).wait_send()
            back(j * split + h).wait_send()
        return carry

    lax.fori_loop(1, chips, finish, 0)

    def finish_core(j, carry):
        for h in range(split):
            forward((2 * j + core) * split + h).wait_send()
            swap((2 * j + 1 - core) * split + h).wait_send()
        return carry

    lax.fori_loop(0, chips, finish_core, 0)

    def finish_chain(t, carry):
        for d in range(2):
            @pl.when(places[d] < depth - 1)
            def _():
                for u in range(SUB):
                    chain(d, t, u).wait_send()

            @pl.when(places[d] > 0)
            def _():
                for u in range(SUB):
                    spread(d, t, u).wait_send()

        return carry

    lax.fori_loop(0, n, finish_chain, 0)
    for k in range(depth):
        @pl.when((z >= k) & (z + 1 < depth))
        def _():
            share(k).wait_send()


def unpack_kernel(pick_ref, scale_ref, rows_ref, context_in, moe_ref, context_out):
    pairs, unit, tile = rows_ref.shape
    mixed = jnp.dot(
        pick_ref[...], rows_ref[...].reshape(pairs * unit, tile), preferred_element_type=jnp.float32
    )
    moe_ref[...] = (mixed * scale_ref[:, :1]).astype(jnp.bfloat16)
    context_out[...] = context_in[...]


def expert_call(ids, features, weight, w_gate, w_up, w_down, queries, latents, ropes, marks, chips, depth, cap):
    seq_len, width = features.shape
    hidden = w_gate.shape[1]
    split = max(1, CHUNKS // (2 * chips))
    group = 2 * chips * split // CHUNKS
    n = CHUNKS
    unit = cap // split
    tall = group * unit
    pairs = chips * split
    query_rows = queries.shape[0]
    heads = queries.shape[1] // (LAT + ROPE)
    lanes = -(-(LAT + ROPE + 1) // 128) * 128
    dma = pltpu.SemaphoreType.DMA
    bf16 = jnp.bfloat16
    vmem = pl.BlockSpec(memory_space=pltpu.VMEM)
    hbm = pl.BlockSpec(memory_space=pl.ANY)
    f32 = jnp.float32
    returned, context, pick, scale = pl.pallas_call(
        functools.partial(expert_kernel, chips, depth, cap, split, group),
        out_shape=(
            jax.ShapeDtypeStruct((pairs, unit, width), bf16),
            jax.ShapeDtypeStruct((query_rows, heads * LAT), bf16),
            jax.ShapeDtypeStruct((seq_len, chips * cap), bf16),
            jax.ShapeDtypeStruct((seq_len, 128), f32),
        ),
        in_specs=[vmem] * 3 + [hbm] * 4 + [vmem] * 3,
        out_specs=(hbm,) * 4,
        scratch_shapes=[
            pltpu.VMEM(w_gate.shape, bf16),
            pltpu.VMEM(w_up.shape, bf16),
            pltpu.VMEM(w_down.shape, bf16),
            pltpu.VMEM(queries.shape, bf16),
            pltpu.VMEM((query_rows, heads * LAT), bf16),
            pltpu.VMEM((seq_len, chips * cap), bf16),
            pltpu.VMEM((seq_len, 128), f32),
            pltpu.VMEM((depth, query_rows, lanes), bf16),
            pltpu.VMEM((2, lanes, depth * query_rows), bf16),
            pltpu.VMEM((query_rows, depth * query_rows), jnp.float32),
            pltpu.VMEM((pairs, unit, width), bf16),
            pltpu.VMEM((n, tall, width), bf16),
            pltpu.VMEM((2 * n, tall, hidden), bf16),
            pltpu.VMEM((2 * n, tall, hidden), bf16),
            pltpu.VMEM((2 * n, tall, hidden // 2), bf16),
            pltpu.VMEM((n, tall, width), bf16),
            pltpu.VMEM((pairs, unit, width), bf16),
            pltpu.VMEM((pairs, unit, width), bf16),
            pltpu.VMEM((2, tall, hidden), jnp.float32),
            dma((pairs,)), dma((pairs,)),
            dma((pairs,)), dma((pairs,)),
            dma((2 * n * SUB,)), dma((2 * n * SUB,)),
            dma((2 * n * SUB,)), dma((2 * n * SUB,)),
            dma((pairs,)), dma((pairs,)),
            dma((pairs,)), dma((pairs,)),
            dma((depth,)), dma((depth,)),
            dma((4,)), dma((3,)), dma((split,)),
        ],
        compiler_params=pltpu.CompilerParams(
            collective_id=0, has_side_effects=True, vmem_limit_bytes=60 << 20
        ),
    )(ids, features, weight, w_gate, w_up, w_down, queries, latents, ropes, marks)
    tile = 896
    steps = width // tile
    context_tile = 3072
    last = context.shape[1] // context_tile - 1
    slab = pl.BlockSpec((query_rows, context_tile), lambda i: (0, jnp.minimum(i, last)))
    return pl.pallas_call(
        unpack_kernel,
        out_shape=(
            jax.ShapeDtypeStruct((seq_len, width), bf16),
            jax.ShapeDtypeStruct(context.shape, bf16),
        ),
        grid=(max(steps, last + 1),),
        in_specs=[
            pl.BlockSpec(pick.shape, lambda i: (0, 0)),
            pl.BlockSpec(scale.shape, lambda i: (0, 0)),
            pl.BlockSpec((pairs, unit, tile), lambda i: (0, 0, jnp.minimum(i, steps - 1))),
            slab,
        ],
        out_specs=(pl.BlockSpec((seq_len, tile), lambda i: (0, jnp.minimum(i, steps - 1))), slab),
    )(pick, scale, returned, context)


def per_device(
    hidden_in, expert_ids, route_weight, w_gate, w_up, w_down, queries, latents, rope_keys, marks
):
    features = hidden_in[0]
    seq_len = features.shape[0]
    slots_per = expert_ids.shape[2]
    chips = lax.axis_size("ep") // 2
    depth = lax.axis_size("ctx")
    capacity = max(2, 3 * seq_len * slots_per // (2 * chips))
    cap = -(-capacity // 16) * 16
    moe, context = expert_call(
        expert_ids[0].reshape(1, -1),
        features,
        route_weight[0].reshape(1, -1),
        w_gate,
        w_up,
        w_down,
        queries[0],
        latents[0],
        jnp.swapaxes(rope_keys, 1, 2)[0],
        marks,
        chips,
        depth,
        cap,
    )
    return (moe[None], context[None])


def solution(mesh):
    placed = (
        P("ep", None, "ctx"),
        P("ep", None, None),
        P("ep", None, None),
        P("ctx", "ep"),
        P("ctx", "ep"),
        P("ep", "ctx"),
        P("ep", "ctx", None),
        P("ep", "ctx", None),
        P("ep", "ctx", None),
        P("ep", "ctx"),
    )
    return jax.shard_map(
        per_device,
        mesh=mesh,
        in_specs=placed,
        out_specs=(P("ep", None, "ctx"), P("ep", "ctx", None)),
        check_vma=False,
    )
```

```python
import functools
import math

import jax
import jax.numpy as jnp
from jax import lax
from jax.experimental import pallas as pl
from jax.experimental.pallas import tpu as pltpu
from jax.sharding import PartitionSpec as P

LAT = 512
ROPE = 64
QK_DIM = 192
CHUNKS = 16
ORDER = (0, 2, 12, 14, 13, 15, 4, 6, 8, 10, 5, 7, 9, 11, 1, 3)
CHAIN = (0, 1, 2, 3)
SPREAD = (6, 5, 4, 3)
SWAP = 2
SUB = 2
LATE = 5
RELAY = (2, 4, 6)
ATTEND = 8
DOWN_FIRST = True
MESH = pl.DeviceIdType.MESH


def flip(a, b, size):
    out = 0
    step = 1
    while step < size:
        out = out + lax.rem(lax.div(a, step) + lax.div(b, step), 2) * step
        step *= 2
    return out


def pick_of(table, i):
    out = table[0]
    for k in range(1, len(table)):
        out = jnp.where(i == k, table[k], out)
    return out


def expert_kernel(
    chips,
    depth,
    cap,
    split,
    group,
    ids_ref,
    feat_ref,
    weight_ref,
    gate_hbm,
    up_hbm,
    down_hbm,
    query_hbm,
    lat_ref,
    rope_ref,
    mark_ref,
    ret_ref,
    ctx_hbm,
    pick_hbm,
    scale_hbm,
    gate_ref,
    up_ref,
    down_ref,
    query_ref,
    ctx_ref,
    pick_ref,
    scale_ref,
    gat_ref,
    keys_ref,
    seen_ref,
    packed,
    rows,
    part_out,
    part_in,
    hid,
    half_out,
    half_in,
    summed,
    acc,
    d_send,
    d_recv,
    f_send,
    f_recv,
    c_send,
    c_recv,
    b_send,
    b_recv,
    h_send,
    h_recv,
    r_send,
    r_recv,
    g_send,
    g_recv,
    in_sem,
    out_sem,
    own_sem,
):
    me = lax.axis_index("ep")
    z = lax.axis_index("ctx")
    core = lax.rem(me, 2)
    chip = lax.div(me, 2)
    sibling = me + 1 - 2 * core
    width = feat_ref.shape[1]
    hidden = gate_ref.shape[1]
    quarter = hidden // 2
    n = CHUNKS
    unit = cap // split

    def block(buf, v):
        if group == 1:
            return buf.at[v]
        start = pl.multiple_of(lax.rem(v, group) * unit, unit)
        return buf.at[lax.div(v, group), pl.ds(start, unit)]

    def pair_of(v):
        return lax.div(v, 2 * split) * split + lax.rem(v, split)

    def core_of(v):
        return lax.rem(lax.div(v, split), 2)

    def remote(src, dst, send, recv, **device):
        return pltpu.make_async_remote_copy(
            src_ref=src, dst_ref=dst, send_sem=send, recv_sem=recv,
            device_id=device, device_id_type=MESH,
        )

    def peer(m):
        return 2 * lax.div(m, split) + core

    def dispatch(m):
        h = lax.rem(m, split)
        return remote(
            packed.at[m], block(rows, me * split + h), d_send.at[m], d_recv.at[chip * split + h], ep=peer(m)
        )

    def arrival(m):
        v = peer(m) * split + lax.rem(m, split)
        return remote(packed.at[m], block(rows, v), d_send.at[m], d_recv.at[m], ep=peer(m))

    def forward(v):
        m = pair_of(v)
        return remote(block(rows, v), block(rows, v), f_send.at[m], f_recv.at[m], ep=sibling)

    nexts = (z + 1, z - 1)
    prevs = (z - 1, z + 1)
    places = (z, depth - 1 - z)

    piece = rows.shape[1] // SUB

    def chain(d, t, u):
        at = d * n + t
        cut = pl.ds(u * piece, piece)
        return remote(
            part_out.at[at, cut], part_in.at[at, cut],
            c_send.at[at * SUB + u], c_recv.at[at * SUB + u], ctx=nexts[d],
        )

    def spread(d, t, u):
        at = d * n + t
        cut = pl.ds(u * piece, piece)
        return remote(
            hid.at[at, cut], hid.at[at, cut],
            b_send.at[at * SUB + u], b_recv.at[at * SUB + u], ctx=prevs[d],
        )

    def swap(v):
        m = pair_of(v)
        return remote(block(half_out, v), half_in.at[m], h_send.at[m], h_recv.at[m], ep=sibling)

    def back(m):
        h = lax.rem(m, split)
        return remote(
            summed.at[m], ret_ref.at[chip * split + h], r_send.at[m], r_recv.at[chip * split + h], ep=peer(m)
        )

    def home(m):
        return remote(summed.at[m], ret_ref.at[m], r_send.at[m], r_recv.at[m], ep=peer(m))

    def share(k):
        return remote(gat_ref.at[z - k], gat_ref.at[z - k], g_send.at[k], g_recv.at[k + 1], ctx=z + 1)

    def shared(k):
        return remote(gat_ref.at[z - k], gat_ref.at[z - k], g_send.at[k], g_recv.at[k], ctx=z - 1)

    def relay(k):
        @pl.when(z >= k)
        def _():
            shared(k).wait_recv()

        @pl.when((z >= k) & (z + 1 < depth))
        def _():
            share(k).start()

    loads = [
        pltpu.make_async_copy(src, dst, in_sem.at[k])
        for k, (src, dst) in enumerate(
            ((gate_hbm, gate_ref), (up_hbm, up_ref), (query_hbm, query_ref), (down_hbm, down_ref))
        )
    ]
    for load in loads:
        load.start()
    stores = [
        pltpu.make_async_copy(src, dst, out_sem.at[k])
        for k, (src, dst) in enumerate(((ctx_ref, ctx_hbm), (pick_ref, pick_hbm), (scale_ref, scale_hbm)))
    ]

    def keep(m):
        return pltpu.make_async_copy(summed.at[m], ret_ref.at[m], own_sem.at[lax.rem(m, split)])

    barrier = pltpu.get_barrier_semaphore()

    def greet(o, carry):
        pl.semaphore_signal(
            barrier, inc=1, device_id={"ep": 2 * flip(chip, o, chips) + core}, device_id_type=MESH
        )
        return carry

    lax.fori_loop(1, chips, greet, 0)
    pl.semaphore_signal(barrier, inc=1, device_id={"ep": sibling}, device_id_type=MESH)

    @pl.when(z > 0)
    def _():
        pl.semaphore_signal(barrier, inc=1, device_id={"ctx": z - 1}, device_id_type=MESH)

    @pl.when(z < depth - 1)
    def _():
        pl.semaphore_signal(barrier, inc=1, device_id={"ctx": z + 1}, device_id_type=MESH)

    bf16, f32 = jnp.bfloat16, jnp.float32
    iota = lax.broadcasted_iota
    query_rows = query_ref.shape[0]
    lanes = gat_ref.shape[2]
    width_k = LAT + ROPE
    eye = iota(jnp.int32, (query_rows, query_rows), 0) == iota(jnp.int32, (query_rows, query_rows), 1)
    mark_col = jnp.sum(jnp.where(eye, mark_ref[...].astype(f32), 0.0), axis=1, keepdims=True)
    for o in range(1, depth):
        @pl.when(o > z)
        def _():
            gat_ref[o] = jnp.zeros((query_rows, lanes), bf16)

    gat_ref[z, :, :LAT] = lat_ref[...]
    gat_ref[z, :, LAT:width_k] = lax.dot_general(
        jnp.where(eye, 1.0, 0.0).astype(bf16), rope_ref[...], (((1,), (1,)), ((), ())),
        preferred_element_type=f32,
    ).astype(bf16)
    gat_ref[z, :, width_k:] = jnp.broadcast_to(mark_col, (query_rows, lanes - width_k)).astype(bf16)

    ids = ids_ref[...]
    tokens = ids.shape[1]
    kinds = max(chips, 16)
    named = iota(jnp.int32, (kinds, tokens), 0) == ids
    earlier = iota(jnp.int32, (tokens, tokens), 0) < iota(jnp.int32, (tokens, tokens), 1)
    counts = jnp.dot(
        jnp.where(named, 1.0, 0.0).astype(bf16),
        jnp.where(earlier, 1.0, 0.0).astype(bf16),
        preferred_element_type=f32,
    )
    rank = jnp.sum(jnp.where(named, counts, 0.0), axis=0, keepdims=True)
    slots = ids * cap + rank.astype(jnp.int32)

    pl.semaphore_wait(barrier, chips + jnp.minimum(z, 1) + jnp.minimum(depth - 1 - z, 1))

    @pl.when(z + 1 < depth)
    def _():
        share(0).start()

    def pack(k, carry):
        o = lax.rem(k + 1, 3) + 1 if chips == 4 else k
        j = flip(chip, o, chips)
        index = j * cap + lax.broadcasted_iota(jnp.int32, (cap, tokens), 0)
        pick = jnp.where(index == slots, 1.0, 0.0).astype(jnp.bfloat16)
        chosen = jnp.dot(pick, feat_ref[...], preferred_element_type=jnp.float32)
        for h in range(split):
            packed[j * split + h] = chosen[h * unit:(h + 1) * unit].astype(bf16)

        @pl.when((o != 2) | (chips != 4))
        def _():
            for h in range(split):
                dispatch(j * split + h).start()

        return carry

    lax.fori_loop(1, chips, pack, 0)
    index = chip * cap + lax.broadcasted_iota(jnp.int32, (cap, tokens), 0)
    pick = jnp.where(index == slots, 1.0, 0.0).astype(jnp.bfloat16)
    chosen = jnp.dot(pick, feat_ref[...], preferred_element_type=jnp.float32)
    for h in range(split):
        block(rows, me * split + h)[...] = chosen[h * unit:(h + 1) * unit].astype(bf16)

    first = lax.div(me * split, group)
    if chips == 4:
        order, swap_lag = ORDER, SWAP
    else:
        order, swap_lag = tuple(range(n)), split
    if depth == 4:
        chain_lag, spread_lag = CHAIN, SPREAD
    else:
        chain_lag = tuple(2 * p for p in range(depth))
        spread_lag = tuple(chain_lag[-1] + 2 * (depth - 1 - p) for p in range(depth))
    chain_at = [pick_of(chain_lag, places[d]) for d in range(2)]
    spread_at = [pick_of(spread_lag, places[d]) for d in range(2)]
    down_lag = spread_lag[0] + 1

    def chunk_at(i):
        return flip(first, pick_of(order, i), n)

    heads = query_ref.shape[1] // width_k
    scale = 1.0 / math.sqrt(QK_DIM)

    def prepare():
        count = depth * query_rows
        keys = gat_ref[...].reshape(count, lanes)
        row = iota(jnp.int32, (lanes, lanes), 0)
        column = iota(jnp.int32, (lanes, lanes), 1)
        even = (row == column) & (row < width_k)
        odd = row == column + (lanes - width_k)
        contract = (((1,), (1,)), ((), ()))
        for a, chosen in ((0, even), (1, odd)):
            pick = jnp.where(chosen, 1.0, 0.0).astype(bf16)
            keys_ref[a] = lax.dot_general(
                pick, keys, contract, preferred_element_type=f32
            ).astype(bf16)
        pick = jnp.where(iota(jnp.int32, (16, lanes), 1) == width_k, 1.0, 0.0).astype(bf16)
        marks = lax.dot_general(pick, keys, contract, preferred_element_type=f32)[:1]
        query_pos = z * query_rows + iota(jnp.int32, (query_rows, count), 0)
        key_pos = iota(jnp.int32, (query_rows, count), 1)
        visible = (key_pos == query_pos) | ((key_pos < query_pos) & (marks < 0.5))
        seen_ref[...] = jnp.where(visible, 0.0, -1e30)

    def attend(pair, a):
        latents = gat_ref[:, :, :LAT].reshape(depth * query_rows, LAT)
        base = pl.multiple_of(pair * (2 * width_k), 128)
        mask = seen_ref[...]
        shift = a * (2 * width_k - lanes)
        q = query_ref[:, pl.ds(pl.multiple_of(base + shift, 128), lanes)]
        scores = jnp.dot(q, keys_ref[a], preferred_element_type=f32) * scale
        masked = jnp.where(mask < 0.0, -1e30, scores)
        top = jnp.max(masked, axis=1, keepdims=True)
        weight = jnp.where(mask < 0.0, 0.0, jnp.exp(masked - top))
        total = jnp.sum(weight, axis=1, keepdims=True)
        acc = jnp.dot(weight.astype(bf16), latents, preferred_element_type=f32)
        where = pl.multiple_of((2 * pair + a) * LAT, 128)
        ctx_ref[:, pl.ds(where, LAT)] = (acc / total).astype(bf16)

    def combine(i):
        t2 = i - down_lag - swap_lag

        @pl.when((t2 >= 0) & (t2 < n))
        def _():
            q = chunk_at(t2)
            for g in range(group):
                v = q * group + g
                m = pair_of(v)
                local = lax.div(m, split) == chip

                @pl.when(core_of(v) == core)
                def _():
                    swap(v).wait_recv()
                    total = block(half_out, v)[...].astype(f32) + half_in[m].astype(f32)
                    summed[m] = total.astype(bf16)

                    @pl.when(jnp.logical_not(local))
                    def _():
                        back(m).start()

                    @pl.when(local)
                    def _():
                        keep(m).start()

    def arrive(i):
        @pl.when(i < n)
        def _():
            q = chunk_at(i)
            for g in range(group):
                v = q * group + g
                mine = core_of(v) == core

                @pl.when(mine & (lax.div(v, 2 * split) != chip))
                def _():
                    arrival(pair_of(v)).wait_recv()

                @pl.when(mine)
                def _():
                    forward(v).start()

            for g in range(group):
                v = q * group + g

                @pl.when(core_of(v) != core)
                def _():
                    forward(v).wait_recv()

    def project(i, d):
        t = i - chain_at[d]
        lo, hi = d * quarter, (d + 1) * quarter

        @pl.when((t >= 0) & (t < n))
        def _():
            q = chunk_at(t)
            at = d * n + t
            x = rows[q]
            gate = jnp.dot(x, gate_ref[:, lo:hi], preferred_element_type=f32)
            up = jnp.dot(x, up_ref[:, lo:hi], preferred_element_type=f32)

            @pl.when(places[d] == 0)
            def _():
                part_out[at, :, :quarter] = gate.astype(bf16)
                part_out[at, :, quarter:] = up.astype(bf16)

            @pl.when(places[d] > 0)
            def _():
                acc[d, :, :quarter] = gate
                acc[d, :, quarter:] = up

    def pass_on(i, d, u):
        t = i - chain_at[d]
        r0, r1 = u * piece, (u + 1) * piece
        at = d * n + t
        live = (t >= 0) & (t < n)

        @pl.when(live & (places[d] == 0))
        def _():
            chain(d, t, u).start()

        @pl.when(live & (places[d] > 0))
        def _():
            chain(d, t, u).wait_recv()
            total = acc[d, r0:r1] + part_in[at, r0:r1].astype(f32)

            @pl.when(places[d] < depth - 1)
            def _():
                part_out[at, r0:r1] = total.astype(bf16)
                chain(d, t, u).start()

            @pl.when(places[d] == depth - 1)
            def _():
                hid[at, r0:r1] = (jax.nn.silu(total[:, :quarter]) * total[:, quarter:]).astype(bf16)
                spread(d, t, u).start()

    def hand_out(i, d, u):
        t = i - spread_at[d]

        @pl.when((t >= 0) & (t < n) & (places[d] < depth - 1))
        def _():
            spread(d, t, u).wait_recv()

            @pl.when(places[d] > 0)
            def _():
                spread(d, t, u).start()

    def lower(i):
        t = i - down_lag

        @pl.when((t >= 0) & (t < n))
        def _():
            q = chunk_at(t)
            h0 = hid[t]
            h1 = hid[n + t]
            tile = 256
            for w in range(0, width, tile):
                got = jnp.dot(h0, down_ref[:quarter, w:w + tile], preferred_element_type=jnp.float32)
                got = got + jnp.dot(
                    h1, down_ref[quarter:, w:w + tile], preferred_element_type=jnp.float32
                )
                half_out[q, :, w:w + tile] = got.astype(jnp.bfloat16)
            for g in range(group):
                v = q * group + g

                @pl.when(core_of(v) != core)
                def _():
                    swap(v).start()

    def place_rows():
        diagonal = iota(jnp.int32, (tokens, tokens), 0) == iota(jnp.int32, (tokens, tokens), 1)
        slot_col = jnp.sum(jnp.where(diagonal, slots, 0), axis=1, keepdims=True)
        weight_col = jnp.sum(jnp.where(diagonal, weight_ref[...], 0.0), axis=1, keepdims=True)
        where = iota(jnp.int32, (tokens, chips * cap), 1) == slot_col
        pick_ref[...] = jnp.where(where, 1.0, 0.0).astype(bf16)
        scale_ref[...] = jnp.broadcast_to(weight_col, scale_ref.shape)
        stores[1].start()
        stores[2].start()

    def step(i, carry):
        @pl.when(i == ATTEND + heads // 2 + 1)
        def _():
            stores[0].start()
            place_rows()

        for k in range(1, depth):
            @pl.when(i == RELAY[k - 1])
            def _():
                relay(k)

        @pl.when(i == ATTEND)
        def _():
            prepare()

        if chips == 4:
            @pl.when(i == LATE)
            def _():
                j = flip(chip, 2, chips)
                for h in range(split):
                    dispatch(j * split + h).start()

        attending = (i > ATTEND) & (i <= ATTEND + heads // 2)
        arrive(i)
        project(i, 0)
        pass_on(i, 0, 0)
        pass_on(i - 1, 1, 1)
        hand_out(i, 0, 0)
        hand_out(i - 1, 1, 1)

        @pl.when(attending)
        def _():
            attend(i - ATTEND - 1, 0)

        combine(i)
        if DOWN_FIRST:
            lower(i)
        project(i, 1)
        pass_on(i, 0, 1)
        pass_on(i, 1, 0)
        hand_out(i, 0, 1)
        hand_out(i, 1, 0)

        @pl.when(attending)
        def _():
            attend(i - ATTEND - 1, 1)

        if not DOWN_FIRST:
            lower(i)
        return carry

    for load in loads:
        load.wait()
    lax.fori_loop(0, max(n + down_lag + swap_lag, ATTEND + 2 + heads // 2), step, 0)

    def land(o, carry):
        for h in range(split):
            home(flip(chip, o, chips) * split + h).wait_recv()
        return carry

    lax.fori_loop(1, chips, land, 0)
    for h in range(split):
        keep(chip * split + h).wait()
    for store in stores:
        store.wait()

    def finish(o, carry):
        j = flip(chip, o, chips)
        for h in range(split):
            dispatch(j * split + h).wait_send()
            back(j * split + h).wait_send()
        return carry

    lax.fori_loop(1, chips, finish, 0)

    def finish_core(j, carry):
        for h in range(split):
            forward((2 * j + core) * split + h).wait_send()
            swap((2 * j + 1 - core) * split + h).wait_send()
        return carry

    lax.fori_loop(0, chips, finish_core, 0)

    def finish_chain(t, carry):
        for d in range(2):
            @pl.when(places[d] < depth - 1)
            def _():
                for u in range(SUB):
                    chain(d, t, u).wait_send()

            @pl.when(places[d] > 0)
            def _():
                for u in range(SUB):
                    spread(d, t, u).wait_send()

        return carry

    lax.fori_loop(0, n, finish_chain, 0)
    for k in range(depth):
        @pl.when((z >= k) & (z + 1 < depth))
        def _():
            share(k).wait_send()


def unpack_kernel(pick_ref, scale_ref, rows_ref, context_in, moe_ref, context_out):
    pairs, unit, tile = rows_ref.shape
    mixed = jnp.dot(
        pick_ref[...], rows_ref[...].reshape(pairs * unit, tile), preferred_element_type=jnp.float32
    )
    moe_ref[...] = (mixed * scale_ref[:, :1]).astype(jnp.bfloat16)
    context_out[...] = context_in[...]


def expert_call(ids, features, weight, w_gate, w_up, w_down, queries, latents, ropes, marks, chips, depth, cap):
    seq_len, width = features.shape
    hidden = w_gate.shape[1]
    split = max(1, CHUNKS // (2 * chips))
    group = 2 * chips * split // CHUNKS
    n = CHUNKS
    unit = cap // split
    tall = group * unit
    pairs = chips * split
    query_rows = queries.shape[0]
    heads = queries.shape[1] // (LAT + ROPE)
    lanes = -(-(LAT + ROPE + 1) // 128) * 128
    dma = pltpu.SemaphoreType.DMA
    bf16 = jnp.bfloat16
    vmem = pl.BlockSpec(memory_space=pltpu.VMEM)
    hbm = pl.BlockSpec(memory_space=pl.ANY)
    f32 = jnp.float32
    returned, context, pick, scale = pl.pallas_call(
        functools.partial(expert_kernel, chips, depth, cap, split, group),
        out_shape=(
            jax.ShapeDtypeStruct((pairs, unit, width), bf16),
            jax.ShapeDtypeStruct((query_rows, heads * LAT), bf16),
            jax.ShapeDtypeStruct((seq_len, chips * cap), bf16),
            jax.ShapeDtypeStruct((seq_len, 128), f32),
        ),
        in_specs=[vmem] * 3 + [hbm] * 4 + [vmem] * 3,
        out_specs=(hbm,) * 4,
        scratch_shapes=[
            pltpu.VMEM(w_gate.shape, bf16),
            pltpu.VMEM(w_up.shape, bf16),
            pltpu.VMEM(w_down.shape, bf16),
            pltpu.VMEM(queries.shape, bf16),
            pltpu.VMEM((query_rows, heads * LAT), bf16),
            pltpu.VMEM((seq_len, chips * cap), bf16),
            pltpu.VMEM((seq_len, 128), f32),
            pltpu.VMEM((depth, query_rows, lanes), bf16),
            pltpu.VMEM((2, lanes, depth * query_rows), bf16),
            pltpu.VMEM((query_rows, depth * query_rows), jnp.float32),
            pltpu.VMEM((pairs, unit, width), bf16),
            pltpu.VMEM((n, tall, width), bf16),
            pltpu.VMEM((2 * n, tall, hidden), bf16),
            pltpu.VMEM((2 * n, tall, hidden), bf16),
            pltpu.VMEM((2 * n, tall, hidden // 2), bf16),
            pltpu.VMEM((n, tall, width), bf16),
            pltpu.VMEM((pairs, unit, width), bf16),
            pltpu.VMEM((pairs, unit, width), bf16),
            pltpu.VMEM((2, tall, hidden), jnp.float32),
            dma((pairs,)), dma((pairs,)),
            dma((pairs,)), dma((pairs,)),
            dma((2 * n * SUB,)), dma((2 * n * SUB,)),
            dma((2 * n * SUB,)), dma((2 * n * SUB,)),
            dma((pairs,)), dma((pairs,)),
            dma((pairs,)), dma((pairs,)),
            dma((depth,)), dma((depth,)),
            dma((4,)), dma((3,)), dma((split,)),
        ],
        compiler_params=pltpu.CompilerParams(
            collective_id=0, has_side_effects=True, vmem_limit_bytes=60 << 20
        ),
    )(ids, features, weight, w_gate, w_up, w_down, queries, latents, ropes, marks)
    tile = 896
    steps = width // tile
    context_tile = 3072
    last = context.shape[1] // context_tile - 1
    slab = pl.BlockSpec((query_rows, context_tile), lambda i: (0, jnp.minimum(i, last)))
    return pl.pallas_call(
        unpack_kernel,
        out_shape=(
            jax.ShapeDtypeStruct((seq_len, width), bf16),
            jax.ShapeDtypeStruct(context.shape, bf16),
        ),
        grid=(max(steps, last + 1),),
        in_specs=[
            pl.BlockSpec(pick.shape, lambda i: (0, 0)),
            pl.BlockSpec(scale.shape, lambda i: (0, 0)),
            pl.BlockSpec((pairs, unit, tile), lambda i: (0, 0, jnp.minimum(i, steps - 1))),
            slab,
        ],
        out_specs=(pl.BlockSpec((seq_len, tile), lambda i: (0, jnp.minimum(i, steps - 1))), slab),
    )(pick, scale, returned, context)


def per_device(
    hidden_in, expert_ids, route_weight, w_gate, w_up, w_down, queries, latents, rope_keys, marks
):
    features = hidden_in[0]
    seq_len = features.shape[0]
    slots_per = expert_ids.shape[2]
    chips = lax.axis_size("ep") // 2
    depth = lax.axis_size("ctx")
    capacity = max(2, 3 * seq_len * slots_per // (2 * chips))
    cap = -(-capacity // 16) * 16
    moe, context = expert_call(
        expert_ids[0].reshape(1, -1),
        features,
        route_weight[0].reshape(1, -1),
        w_gate,
        w_up,
        w_down,
        queries[0],
        latents[0],
        jnp.swapaxes(rope_keys, 1, 2)[0],
        marks,
        chips,
        depth,
        cap,
    )
    return (moe[None], context[None])


def solution(mesh):
    placed = (
        P("ep", None, "ctx"),
        P("ep", None, None),
        P("ep", None, None),
        P("ctx", "ep"),
        P("ctx", "ep"),
        P("ep", "ctx"),
        P("ep", "ctx", None),
        P("ep", "ctx", None),
        P("ep", "ctx", None),
        P("ep", "ctx"),
    )
    return jax.shard_map(
        per_device,
        mesh=mesh,
        in_specs=placed,
        out_specs=(P("ep", None, "ctx"), P("ep", "ctx", None)),
        check_vma=False,
    )
```
